512 devices in a mesh: seq: 128 (over x, y_lo, z, core), head: 4 (over y_hi).
Axes of the slice: x: 4, y: 8 (y_hi: 4, y_lo: 2; y = y_hi * 2 + y_lo), z: 8, core: 2. Of those that a mesh axis runs over, the one named last changes fastest.
Arguments:
- query_rows: bfloat16 [65536, 2048], P(('seq', 'head')), may hold values from -48 to 48
- key_rows: bfloat16 [65536, 1024], P(('seq', 'head')), may hold values from -16 to 16
- saved_value_rows: bfloat16 [65536, 1024], P(('seq', 'head')), may hold values from -6 to 6
- out_grad: bfloat16 [65536, 2048], P(('seq', 'head')), may hold values from -6 to 6
Outputs:
- query_grad: bfloat16 [65536, 2048], P(('seq', 'head'))
- key_grad: bfloat16 [65536, 1024], P(('seq', 'head'))
- value_grad: bfloat16 [65536, 1024], P(('seq', 'head'))
The draws below stay inside these ranges and needn't reach their ends.
All inputs are finite; a program needn't handle non-finite values.
Results may differ from the reference program's by a relative error of at most 0.013.
Values may be sent and summed in bfloat16 or wider, within the bound.
A program may use at most 64 MiB of HBM per device.

```python
import jax
import jax.numpy as jnp
from jax import lax

HQ = 16
KEY_VALUE_HEADS = 8
HEAD_SIZE = 128
W = 1024
SHARD_POSITIONS = 512
SEQUENCE_TOKENS = 65536
N_SEQ = 128


def draw_query_rows(key, part):
    drawn_result = jnp.clip(jax.random.normal(jax.random.fold_in(key, 202), (SEQUENCE_TOKENS, HQ, HEAD_SIZE), jnp.float32), -6.0, 6.0)
    return drawn_result.reshape(SEQUENCE_TOKENS, HQ * HEAD_SIZE).astype(jnp.bfloat16)


def draw_key_rows(key, part):
    drawn_result = jnp.clip(jax.random.normal(jax.random.fold_in(key, 302), (SEQUENCE_TOKENS, KEY_VALUE_HEADS, HEAD_SIZE), jnp.float32), -6.0, 6.0)
    return drawn_result.reshape(SEQUENCE_TOKENS, KEY_VALUE_HEADS * HEAD_SIZE).astype(jnp.bfloat16)


def steps_of(own_key, shape, cuts, least, largest):
    def one(dim, blocks):
        steps = jax.random.uniform(jax.random.fold_in(jax.random.fold_in(own_key, 6), dim), (blocks,), jnp.float32, least / len(cuts), largest / len(cuts))
        return jnp.repeat(jnp.exp(steps), shape[dim] // blocks).reshape((-1,) + (1,) * (len(shape) - dim - 1))

    loudness = one(*cuts[0])
    for cut in cuts[1:]:
        loudness = loudness * one(*cut)
    return loudness


def scatter_about(stream_key, shape, deviation, limit, pieces=(), held_as=jnp.bfloat16):
    result = deviation * jax.random.normal(stream_key, shape, jnp.float32)
    if pieces:
        result = result * steps_of(stream_key, shape, pieces, -0.22, 0.18)
    return jnp.clip(result, -limit, limit).astype(held_as)


def setup_inputs(seed: int = 0) -> dict:
    streams_of = jax.random.split(jax.random.key(seed), 5)
    return {
        "query_rows": draw_query_rows(jax.random.fold_in(streams_of[4], 71), 0),
        "key_rows": draw_key_rows(jax.random.fold_in(streams_of[4], 71), 0),
        "saved_value_rows": scatter_about(streams_of[2], (SEQUENCE_TOKENS, KEY_VALUE_HEADS * HEAD_SIZE), 1.0, 6.0, ((0, 512),)),
        "out_grad": scatter_about(streams_of[3], (SEQUENCE_TOKENS, HQ * HEAD_SIZE), 1.0, 6.0, ((0, 512),)),
    }


score_scale = 168.0 ** -0.5
masked_value = -1.0e30


def reference(query_rows, key_rows, saved_value_rows, out_grad):
    empty_rows = jnp.zeros((2 * SHARD_POSITIONS, KEY_VALUE_HEADS * HEAD_SIZE), jnp.bfloat16)
    padded_keys = jnp.concatenate([empty_rows, key_rows], 0)
    padded_values = jnp.concatenate([empty_rows, saved_value_rows], 0)

    def block_step(carry, block):
        key_acc, value_acc = carry
        start_offset = (block * SHARD_POSITIONS).astype(jnp.int32)
        query_block = lax.dynamic_slice_in_dim(query_rows, start_offset, SHARD_POSITIONS, 0).reshape(SHARD_POSITIONS, HQ, HEAD_SIZE).astype(jnp.float32)
        grad_block = lax.dynamic_slice_in_dim(out_grad, start_offset, SHARD_POSITIONS, 0).reshape(SHARD_POSITIONS, HQ, HEAD_SIZE).astype(jnp.float32)
        key_tile_block = lax.dynamic_slice_in_dim(padded_keys, start_offset, 3 * SHARD_POSITIONS, 0).reshape(3 * SHARD_POSITIONS, KEY_VALUE_HEADS, HEAD_SIZE)
        value_tile_block = lax.dynamic_slice_in_dim(padded_values, start_offset, 3 * SHARD_POSITIONS, 0).reshape(3 * SHARD_POSITIONS, KEY_VALUE_HEADS, HEAD_SIZE)
        key_heads = jnp.repeat(key_tile_block, 2, axis=1).astype(jnp.float32)
        value_heads = jnp.repeat(value_tile_block, 2, axis=1).astype(jnp.float32)
        query_pos = start_offset + jnp.arange(SHARD_POSITIONS, dtype=jnp.int32)
        key_pos = start_offset - 2 * SHARD_POSITIONS + jnp.arange(3 * SHARD_POSITIONS, dtype=jnp.int32)
        distance = query_pos[:, None] - key_pos[None, :]
        visible = (distance >= 0) & (distance < W) & (key_pos[None, :] >= 0)
        scores = jnp.einsum("qhd,khd->hqk", query_block, key_heads) * score_scale
        scores = jnp.where(visible[None], scores, masked_value)
        row_max = jnp.max(scores, axis=2, keepdims=True)
        weights = jnp.exp(scores - row_max)
        attention = weights / jnp.sum(weights, axis=2, keepdims=True)
        attention_low = attention.astype(jnp.bfloat16)
        prob_grad = jnp.einsum("qhd,khd->hqk", grad_block, value_heads)
        row_delta = jnp.sum(attention * prob_grad, axis=2, keepdims=True)
        score_grad = (score_scale * attention * (prob_grad - row_delta)).astype(jnp.bfloat16)
        query_part = jnp.einsum("hqk,khd->qhd", score_grad.astype(jnp.float32), key_heads)
        query_part = query_part.astype(jnp.bfloat16).reshape(SHARD_POSITIONS, HQ * HEAD_SIZE)
        key_portion = jnp.einsum("hqk,qhd->khd", score_grad.astype(jnp.float32), query_block)
        key_portion = key_portion.reshape(3 * SHARD_POSITIONS, KEY_VALUE_HEADS, 2, HEAD_SIZE).sum(axis=2).reshape(3 * SHARD_POSITIONS, KEY_VALUE_HEADS * HEAD_SIZE)
        value_portion = jnp.einsum("hqk,qhd->khd", attention_low.astype(jnp.float32), grad_block)
        value_portion = value_portion.reshape(3 * SHARD_POSITIONS, KEY_VALUE_HEADS, 2, HEAD_SIZE).sum(axis=2).reshape(3 * SHARD_POSITIONS, KEY_VALUE_HEADS * HEAD_SIZE)
        key_old = lax.dynamic_slice_in_dim(key_acc, start_offset, 3 * SHARD_POSITIONS, 0)
        value_old = lax.dynamic_slice_in_dim(value_acc, start_offset, 3 * SHARD_POSITIONS, 0)
        key_acc = lax.dynamic_update_slice_in_dim(key_acc, key_old + key_portion, start_offset, 0)
        value_acc = lax.dynamic_update_slice_in_dim(value_acc, value_old + value_portion, start_offset, 0)
        return (key_acc, value_acc), query_part

    start_accumulator = jnp.zeros((SEQUENCE_TOKENS + 2 * SHARD_POSITIONS, KEY_VALUE_HEADS * HEAD_SIZE), jnp.float32)
    (key_acc, value_acc), query_parts = lax.scan(block_step, (start_accumulator, start_accumulator), jnp.arange(N_SEQ, dtype=jnp.int32))
    query_grad = query_parts.reshape(SEQUENCE_TOKENS, HQ * HEAD_SIZE)
    key_grad = key_acc[2 * SHARD_POSITIONS:].astype(jnp.bfloat16)
    value_grad = value_acc[2 * SHARD_POSITIONS:].astype(jnp.bfloat16)
    return (query_grad, key_grad, value_grad)
```

```python
import jax
import jax.numpy as jnp
from jax import lax
from jax.experimental import pallas as pl
from jax.experimental.pallas import tpu as pltpu
from jax.sharding import PartitionSpec as P

HEAD_SIZE = 128
W = 1024
PEERS = 8
BLOCK = W // PEERS
QUERIES = 256
STEPS = W // QUERIES
CHUNK = 256
CHUNKS = (W + QUERIES) // CHUNK
MESH = pl.DeviceIdType.MESH

score_scale = 168.0 ** (-0.5)
masked_value = -1e30
contract_last = (((1,), (1,)), ((), ()))

OTHERS = ((1, 0), (3, 0), (2, 0), (1, 1), (3, 1), (2, 1), (0, 1))
K, V, Q0, G0, Q1, G1 = range(6)


def kernel(
    query_in,
    key_in,
    value_in,
    grad_in,
    query_out,
    key_out,
    value_out,
    keys,
    values,
    keys_t,
    queries,
    grads,
    key_sum,
    value_sum,
    query_stage,
    back_stage,
    back_landing,
    own_stage,
    score_buf,
    prob_buf,
    in_send,
    in_recv,
    halo_send,
    halo_recv,
    query_send,
    query_recv,
    back_send,
    back_recv,
    own_send,
    own_recv,
):
    seq_count = lax.axis_size("seq")
    seq = lax.axis_index("seq")
    head = lax.axis_index("head")
    span = seq // 2
    core = seq % 2
    me = core * 4 + head

    def peer(step):
        other_head = (head + step[0]) % 4
        other_core = (core + step[1]) % 2
        return other_core * 4 + other_head, {"seq": span * 2 + other_core, "head": other_head}

    peers = [peer(step) for step in OTHERS]
    following = {"seq": (seq + 2) % seq_count, "head": head}
    preceding = {"seq": (seq + seq_count - 2) % seq_count, "head": head}

    def rows(block, size=BLOCK):
        return pl.ds(pl.multiple_of(block * size, size), size)

    def columns(index):
        return pl.ds(pl.multiple_of(index * HEAD_SIZE, HEAD_SIZE), HEAD_SIZE)

    def source(kind, home):
        if kind == K:
            return key_in.at[:, columns(home)]
        if kind == V:
            return value_in.at[:, columns(home)]
        array = query_in if kind in (Q0, Q1) else grad_in
        return array.at[:, columns(2 * home + (1 if kind in (Q1, G1) else 0))]

    def landing(kind, block):
        if kind == K:
            return keys.at[rows(PEERS + block)]
        if kind == V:
            return values.at[rows(PEERS + block)]
        array = queries if kind in (Q0, Q1) else grads
        return array.at[1 if kind in (Q1, G1) else 0, rows(block)]

    def local_in(kind):
        return pltpu.make_async_copy(source(kind, me), landing(kind, me), in_recv.at[kind, me])

    def remote_in(kind, index, device, block):
        return pltpu.make_async_remote_copy(
            src_ref=source(kind, index),
            dst_ref=landing(kind, block),
            send_sem=in_send.at[kind, index],
            recv_sem=in_recv.at[kind, block],
            device_id=device,
            device_id_type=MESH,
        )

    def wait_in(kind):
        for index, device in peers:
            remote_in(kind, index, device, index).wait_recv()
        local_in(kind).wait()

    for kind in (K, V, Q0, G0, Q1, G1):
        local_in(kind).start()

    barrier = pltpu.get_barrier_semaphore()
    for device in [device for _, device in peers] + [following, preceding]:
        pl.semaphore_signal(barrier, inc=1, device_id=device, device_id_type=MESH)
    pl.semaphore_wait(barrier, len(OTHERS) + 2)

    for kind in (K, V, Q0, G0, Q1, G1):
        for index, device in peers:
            remote_in(kind, index, device, me).start()

    key_sum[...] = jnp.zeros_like(key_sum)
    value_sum[...] = jnp.zeros_like(value_sum)

    def halo(which):
        array = keys if which == 0 else values
        return pltpu.make_async_remote_copy(
            src_ref=array.at[pl.ds(W, W)],
            dst_ref=array.at[pl.ds(0, W)],
            send_sem=halo_send.at[which],
            recv_sem=halo_recv.at[which],
            device_id=following,
            device_id_type=MESH,
        )

    wait_in(K)
    halo(0).start()
    wait_in(V)
    halo(1).start()
    halo(0).wait_recv()

    @pl.loop(0, 2 * W // CHUNK)
    def _(chunk):
        keys_t[chunk] = keys[rows(chunk, CHUNK), :].T

    halo(1).wait_recv()

    key_row = lax.broadcasted_iota(jnp.int32, (CHUNK, QUERIES), 0)
    query_row = lax.broadcasted_iota(jnp.int32, (CHUNK, QUERIES), 1)

    def compute(q_head, step):
        query = queries[q_head, rows(step, QUERIES), :]
        grad = grads[q_head, rows(step, QUERIES), :]
        peak = None
        for part in range(CHUNKS):
            scores = (
                lax.dot_general(
                    keys[rows(step + part, CHUNK), :],
                    query,
                    contract_last,
                    preferred_element_type=jnp.float32,
                )
                * score_scale
            )
            if part < CHUNKS - 1:
                absent = (span == 0) & (step + part < W // CHUNK)
                scores = scores + jnp.where(absent, masked_value, 0.0)
            if part == 0:
                scores = jnp.where(key_row > query_row, scores, masked_value)
            if part == CHUNKS - 1:
                scores = jnp.where(key_row <= query_row, scores, masked_value)
            score_buf[part] = scores
            top = jnp.max(scores, axis=0, keepdims=True)
            peak = top if peak is None else jnp.maximum(peak, top)
        total = jnp.zeros((1, QUERIES), jnp.float32)
        delta = jnp.zeros((1, QUERIES), jnp.float32)
        for part in range(CHUNKS):
            weights = jnp.exp(score_buf[part] - peak)
            prob_grad = lax.dot_general(
                values[rows(step + part, CHUNK), :],
                grad,
                contract_last,
                preferred_element_type=jnp.float32,
            )
            score_buf[part] = weights
            prob_buf[part] = prob_grad
            total = total + jnp.sum(weights, axis=0, keepdims=True)
            delta = delta + jnp.sum(weights * prob_grad, axis=0, keepdims=True)
        inverse = 1.0 / total
        delta = delta * inverse
        query_grad = jnp.zeros((HEAD_SIZE, QUERIES), jnp.float32)
        for part in range(CHUNKS):
            attention = score_buf[part] * inverse
            score_grad = (score_scale * attention * (prob_buf[part] - delta)).astype(jnp.bfloat16)
            at = rows(step + part, CHUNK)
            value_sum[at, :] += jnp.dot(
                attention.astype(jnp.bfloat16), grad, preferred_element_type=jnp.float32
            )
            key_sum[at, :] += jnp.dot(score_grad, query, preferred_element_type=jnp.float32)
            query_grad = query_grad + jnp.dot(
                keys_t[step + part], score_grad, preferred_element_type=jnp.float32
            )
        query_stage[q_head, rows(step, QUERIES), :] = query_grad.T.astype(jnp.bfloat16)

    def query_local(q_head):
        return pltpu.make_async_copy(
            query_stage.at[q_head, rows(me)],
            query_out.at[:, columns(2 * me + q_head)],
            query_recv.at[q_head, me],
        )

    def query_remote(q_head, index, device, home):
        return pltpu.make_async_remote_copy(
            src_ref=query_stage.at[q_head, rows(index)],
            dst_ref=query_out.at[:, columns(2 * home + q_head)],
            send_sem=query_send.at[q_head, index],
            recv_sem=query_recv.at[q_head, home],
            device_id=device,
            device_id_type=MESH,
        )

    def send_query(q_head):
        query_local(q_head).start()
        for index, device in peers:
            query_remote(q_head, index, device, me).start()

    def back(which, step):
        return pltpu.make_async_remote_copy(
            src_ref=back_stage.at[which, rows(step, QUERIES)],
            dst_ref=back_landing.at[which, rows(step, QUERIES)],
            send_sem=back_send.at[which, step],
            recv_sem=back_recv.at[which, step],
            device_id=preceding,
            device_id_type=MESH,
        )

    wait_in(Q0)
    wait_in(G0)

    @pl.loop(0, STEPS)
    def _(step):
        compute(0, step)

    wait_in(Q1)
    wait_in(G1)
    send_query(0)

    @pl.loop(0, STEPS)
    def _(step):
        compute(1, step)
        at = rows(step, QUERIES)
        back_stage[0, at, :] = key_sum[at, :].astype(jnp.bfloat16)
        back_stage[1, at, :] = value_sum[at, :].astype(jnp.bfloat16)
        back(0, step).start()
        back(1, step).start()

    send_query(1)

    def own_out(which):
        return key_out if which == 0 else value_out

    def own_local(which):
        return pltpu.make_async_copy(
            own_stage.at[which, rows(me)],
            own_out(which).at[:, columns(me)],
            own_recv.at[which, me],
        )

    def own_remote(which, index, device, home):
        return pltpu.make_async_remote_copy(
            src_ref=own_stage.at[which, rows(index)],
            dst_ref=own_out(which).at[:, columns(home)],
            send_sem=own_send.at[which, index],
            recv_sem=own_recv.at[which, home],
            device_id=device,
            device_id_type=MESH,
        )

    @pl.loop(0, STEPS)
    def _(step):
        at = rows(step, QUERIES)
        own = rows(STEPS + step, QUERIES)
        for which, sums in ((0, key_sum), (1, value_sum)):
            back(which, step).wait_recv()
            own_stage[which, at, :] = (
                sums[own, :] + back_landing[which, at, :].astype(jnp.float32)
            ).astype(jnp.bfloat16)

    for which in (0, 1):
        own_local(which).start()
        for index, device in peers:
            own_remote(which, index, device, me).start()

    for kind in (K, V, Q0, G0, Q1, G1):
        for index, device in peers:
            remote_in(kind, index, device, me).wait_send()
    for which in (0, 1):
        halo(which).wait_send()
        for step in range(STEPS):
            back(which, step).wait_send()
        query_local(which).wait()
        own_local(which).wait()
        for index, device in peers:
            query_remote(which, index, device, me).wait_send()
            query_remote(which, index, device, index).wait_recv()
            own_remote(which, index, device, me).wait_send()
            own_remote(which, index, device, index).wait_recv()


def on_device(query_rows, key_rows, saved_value_rows, out_grad):
    dma = pltpu.SemaphoreType.DMA
    low, wide = jnp.bfloat16, jnp.float32
    anywhere = pl.BlockSpec(memory_space=pl.ANY)
    return pl.pallas_call(
        kernel,
        out_shape=(
            jax.ShapeDtypeStruct(query_rows.shape, low),
            jax.ShapeDtypeStruct(key_rows.shape, low),
            jax.ShapeDtypeStruct(saved_value_rows.shape, low),
        ),
        in_specs=[anywhere] * 4,
        out_specs=(anywhere,) * 3,
        scratch_shapes=[
            pltpu.VMEM((2 * W, HEAD_SIZE), low),
            pltpu.VMEM((2 * W, HEAD_SIZE), low),
            pltpu.VMEM((2 * W // CHUNK, HEAD_SIZE, CHUNK), low),
            pltpu.VMEM((2, W, HEAD_SIZE), low),
            pltpu.VMEM((2, W, HEAD_SIZE), low),
            pltpu.VMEM((2 * W, HEAD_SIZE), wide),
            pltpu.VMEM((2 * W, HEAD_SIZE), wide),
            pltpu.VMEM((2, W, HEAD_SIZE), low),
            pltpu.VMEM((2, W, HEAD_SIZE), low),
            pltpu.VMEM((2, W, HEAD_SIZE), low),
            pltpu.VMEM((2, W, HEAD_SIZE), low),
            pltpu.VMEM((CHUNKS, CHUNK, QUERIES), wide),
            pltpu.VMEM((CHUNKS, CHUNK, QUERIES), wide),
            dma((6, PEERS)),
            dma((6, PEERS)),
            dma((2,)),
            dma((2,)),
            dma((2, PEERS)),
            dma((2, PEERS)),
            dma((2, STEPS)),
            dma((2, STEPS)),
            dma((2, PEERS)),
            dma((2, PEERS)),
        ],
        compiler_params=pltpu.CompilerParams(collective_id=0, has_side_effects=True),
        name="attention_backward",
    )(query_rows, key_rows, saved_value_rows, out_grad)


def solution(mesh):
    rows_split = P(("seq", "head"), None)
    return jax.shard_map(
        on_device,
        mesh=mesh,
        in_specs=(rows_split,) * 4,
        out_specs=(rows_split,) * 3,
        check_vma=False,
    )
```

```python
import jax
import jax.numpy as jnp
from jax import lax
from jax.experimental import pallas as pl
from jax.experimental.pallas import tpu as pltpu
from jax.sharding import PartitionSpec as P

HEAD_SIZE = 128
W = 1024
BLOCKS = 8
BLOCK = W // BLOCKS
LINE = 8
DEPTH = 8
QUERIES = 256
STEPS = W // QUERIES
CHUNK = 256
CHUNKS = (W + QUERIES) // CHUNK
MESH = pl.DeviceIdType.MESH

score_scale = 168.0 ** (-0.5)
masked_value = -1e30
contract_last = (((1,), (1,)), ((), ()))

HOMES = (1, 7, 2, 6, 3, 5, 4)
OWNERS = ((0, 1), (1, 1), (0, 3), (1, 3), (0, 2), (1, 2), (1, 0))
KINDS = K, V, Q0, G0, Q1, G1 = range(6)


def kernel(
    query_in,
    key_in,
    value_in,
    grad_in,
    query_out,
    key_out,
    value_out,
    keys,
    values,
    keys_t,
    queries,
    grads,
    key_sum,
    value_sum,
    query_stage,
    back_stage,
    back_landing,
    own_stage,
    score_buf,
    prob_buf,
    in_send,
    in_recv,
    halo_send,
    halo_recv,
    query_send,
    query_recv,
    back_send,
    back_recv,
    own_send,
    own_recv,
):
    seq = lax.axis_index("seq")
    head = lax.axis_index("head")
    core = seq % 2
    z = seq // 2 % DEPTH
    y_lo = seq // (2 * DEPTH) % 2
    x = seq // (4 * DEPTH)
    y = head * 2 + y_lo
    mine = core * 4 + head
    alone = core == y_lo
    span = (x * 2 + core) * DEPTH + z
    span_count = lax.axis_size("seq") // 2

    def chip(other_y, other_core):
        other = (x * 2 + other_y % 2) * (2 * DEPTH) + z * 2 + other_core
        return {"seq": other, "head": other_y // 2}

    def span_home(other):
        place = (other // (2 * DEPTH) * 2 + y_lo) * (2 * DEPTH) + other % DEPTH * 2
        return {"seq": place + other // DEPTH % 2, "head": head}

    def owner(step):
        block_core, place = (core + step[0]) % 2, (head + step[1]) % 4
        return block_core * 4 + place, chip(place * 2 + core, block_core)

    homes = [((y + step) % LINE, chip((y + step) % LINE, y_lo)) for step in HOMES]
    owners = [owner(step) for step in OWNERS]
    near_home = (y, chip(y, y_lo))
    near_owner = owner((0, 0))
    following = span_home((span + 1) % span_count)
    preceding = span_home((span + span_count - 1) % span_count)

    def rows(block, size=BLOCK):
        return pl.ds(pl.multiple_of(block * size, size), size)

    def columns(index):
        return pl.ds(pl.multiple_of(index * HEAD_SIZE, HEAD_SIZE), HEAD_SIZE)

    def source(kind, home):
        if kind == K:
            return key_in.at[:, columns(home)]
        if kind == V:
            return value_in.at[:, columns(home)]
        array = query_in if kind in (Q0, Q1) else grad_in
        return array.at[:, columns(2 * home + (1 if kind in (Q1, G1) else 0))]

    def landing(kind, block):
        if kind == K:
            return keys.at[rows(BLOCKS + block)]
        if kind == V:
            return values.at[rows(BLOCKS + block)]
        array = queries if kind in (Q0, Q1) else grads
        return array.at[1 if kind in (Q1, G1) else 0, rows(block)]

    def local_in(kind):
        return pltpu.make_async_copy(source(kind, y), landing(kind, mine), in_recv.at[kind, mine])

    def remote_in(kind, home, device, block):
        return pltpu.make_async_remote_copy(
            src_ref=source(kind, home),
            dst_ref=landing(kind, block),
            send_sem=in_send.at[kind, home],
            recv_sem=in_recv.at[kind, block],
            device_id=device,
            device_id_type=MESH,
        )

    def wait_in(kind):
        for block, device in owners + [near_owner]:
            remote_in(kind, y, device, block).wait_recv()

    @pl.when(alone)
    def _():
        for kind in KINDS:
            local_in(kind).start()

    barrier = pltpu.get_barrier_semaphore()

    def greet(device):
        pl.semaphore_signal(barrier, inc=1, device_id=device, device_id_type=MESH)

    for _, device in homes:
        greet(device)
    for place in range(4):
        greet(chip(place * 2 + core, 1 - y_lo))
    greet(following)
    greet(preceding)

    @pl.when(jnp.logical_not(alone))
    def _():
        greet(near_home[1])

    pl.semaphore_wait(barrier, len(homes) + 6 + jnp.where(alone, 0, 1))

    for kind in KINDS:
        for home, device in homes:
            remote_in(kind, home, device, mine).start()

        @pl.when(jnp.logical_not(alone))
        def _():
            remote_in(kind, *near_home, mine).start()

    key_sum[...] = jnp.zeros_like(key_sum)
    value_sum[...] = jnp.zeros_like(value_sum)

    def halo(which):
        array = keys if which == 0 else values
        return pltpu.make_async_remote_copy(
            src_ref=array.at[pl.ds(W, W)],
            dst_ref=array.at[pl.ds(0, W)],
            send_sem=halo_send.at[which],
            recv_sem=halo_recv.at[which],
            device_id=following,
            device_id_type=MESH,
        )

    wait_in(K)
    halo(0).start()
    wait_in(V)
    halo(1).start()
    halo(0).wait_recv()

    @pl.loop(0, 2 * W // CHUNK)
    def _(chunk):
        keys_t[chunk] = keys[rows(chunk, CHUNK), :].T

    halo(1).wait_recv()

    key_row = lax.broadcasted_iota(jnp.int32, (CHUNK, QUERIES), 0)
    query_row = lax.broadcasted_iota(jnp.int32, (CHUNK, QUERIES), 1)

    def compute(q_head, step):
        query = queries[q_head, rows(step, QUERIES), :]
        grad = grads[q_head, rows(step, QUERIES), :]
        peak = None
        for part in range(CHUNKS):
            scores = (
                lax.dot_general(
                    keys[rows(step + part, CHUNK), :],
                    query,
                    contract_last,
                    preferred_element_type=jnp.float32,
                )
                * score_scale
            )
            if part < CHUNKS - 1:
                absent = (span == 0) & (step + part < W // CHUNK)
                scores = scores + jnp.where(absent, masked_value, 0.0)
            if part == 0:
                scores = jnp.where(key_row > query_row, scores, masked_value)
            if part == CHUNKS - 1:
                scores = jnp.where(key_row <= query_row, scores, masked_value)
            score_buf[part] = scores
            top = jnp.max(scores, axis=0, keepdims=True)
            peak = top if peak is None else jnp.maximum(peak, top)
        total = jnp.zeros((1, QUERIES), jnp.float32)
        delta = jnp.zeros((1, QUERIES), jnp.float32)
        for part in range(CHUNKS):
            weights = jnp.exp(score_buf[part] - peak)
            prob_grad = lax.dot_general(
                values[rows(step + part, CHUNK), :],
                grad,
                contract_last,
                preferred_element_type=jnp.float32,
            )
            score_buf[part] = weights
            prob_buf[part] = prob_grad
            total = total + jnp.sum(weights, axis=0, keepdims=True)
            delta = delta + jnp.sum(weights * prob_grad, axis=0, keepdims=True)
        inverse = 1.0 / total
        delta = delta * inverse
        query_grad = jnp.zeros((HEAD_SIZE, QUERIES), jnp.float32)
        for part in range(CHUNKS):
            attention = score_buf[part] * inverse
            score_grad = (score_scale * attention * (prob_buf[part] - delta)).astype(jnp.bfloat16)
            at = rows(step + part, CHUNK)
            value_sum[at, :] += jnp.dot(
                attention.astype(jnp.bfloat16), grad, preferred_element_type=jnp.float32
            )
            key_sum[at, :] += jnp.dot(score_grad, query, preferred_element_type=jnp.float32)
            query_grad = query_grad + jnp.dot(
                keys_t[step + part], score_grad, preferred_element_type=jnp.float32
            )
        query_stage[q_head, rows(step, QUERIES), :] = query_grad.T.astype(jnp.bfloat16)

    def query_local(q_head):
        return pltpu.make_async_copy(
            query_stage.at[q_head, rows(mine)],
            query_out.at[:, columns(2 * y + q_head)],
            query_recv.at[q_head, y],
        )

    def query_remote(q_head, block, device, home):
        return pltpu.make_async_remote_copy(
            src_ref=query_stage.at[q_head, rows(block)],
            dst_ref=query_out.at[:, columns(2 * home + q_head)],
            send_sem=query_send.at[q_head, block],
            recv_sem=query_recv.at[q_head, home],
            device_id=device,
            device_id_type=MESH,
        )

    def send_query(q_head):
        for block, device in owners:
            query_remote(q_head, block, device, y).start()

        @pl.when(alone)
        def _():
            query_local(q_head).start()

        @pl.when(jnp.logical_not(alone))
        def _():
            query_remote(q_head, *near_owner, y).start()

    def back(which, step):
        return pltpu.make_async_remote_copy(
            src_ref=back_stage.at[which, rows(step, QUERIES)],
            dst_ref=back_landing.at[which, rows(step, QUERIES)],
            send_sem=back_send.at[which, step],
            recv_sem=back_recv.at[which, step],
            device_id=preceding,
            device_id_type=MESH,
        )

    wait_in(Q0)
    wait_in(G0)

    @pl.loop(0, STEPS)
    def _(step):
        compute(0, step)

    wait_in(Q1)
    wait_in(G1)
    send_query(0)

    @pl.loop(0, STEPS)
    def _(step):
        compute(1, step)
        at = rows(step, QUERIES)
        back_stage[0, at, :] = key_sum[at, :].astype(jnp.bfloat16)
        back_stage[1, at, :] = value_sum[at, :].astype(jnp.bfloat16)
        back(0, step).start()
        back(1, step).start()

    send_query(1)

    def own_out(which):
        return key_out if which == 0 else value_out

    def own_local(which):
        return pltpu.make_async_copy(
            own_stage.at[which, rows(mine)],
            own_out(which).at[:, columns(y)],
            own_recv.at[which, y],
        )

    def own_remote(which, block, device, home):
        return pltpu.make_async_remote_copy(
            src_ref=own_stage.at[which, rows(block)],
            dst_ref=own_out(which).at[:, columns(home)],
            send_sem=own_send.at[which, block],
            recv_sem=own_recv.at[which, home],
            device_id=device,
            device_id_type=MESH,
        )

    @pl.loop(0, STEPS)
    def _(step):
        at = rows(step, QUERIES)
        own = rows(STEPS + step, QUERIES)
        for which, sums in ((0, key_sum), (1, value_sum)):
            back(which, step).wait_recv()
            own_stage[which, at, :] = (
                sums[own, :] + back_landing[which, at, :].astype(jnp.float32)
            ).astype(jnp.bfloat16)

    for which in (0, 1):
        for block, device in owners:
            own_remote(which, block, device, y).start()

    @pl.when(alone)
    def _():
        for which in (0, 1):
            own_local(which).start()

    @pl.when(jnp.logical_not(alone))
    def _():
        for which in (0, 1):
            own_remote(which, *near_owner, y).start()
        for kind in KINDS:
            remote_in(kind, *near_home, mine).wait_send()
        for which in (0, 1):
            query_remote(which, *near_owner, y).wait_send()
            own_remote(which, *near_owner, y).wait_send()

    for kind in KINDS:
        for home, device in homes:
            remote_in(kind, home, device, mine).wait_send()
    for which in (0, 1):
        halo(which).wait_send()
        for step in range(STEPS):
            back(which, step).wait_send()
        for block, device in owners:
            query_remote(which, block, device, y).wait_send()
            own_remote(which, block, device, y).wait_send()
        for home, device in homes + [near_home]:
            query_remote(which, mine, device, home).wait_recv()
            own_remote(which, mine, device, home).wait_recv()


def on_device(query_rows, key_rows, saved_value_rows, out_grad):
    dma = pltpu.SemaphoreType.DMA
    low, wide = jnp.bfloat16, jnp.float32
    anywhere = pl.BlockSpec(memory_space=pl.ANY)
    return pl.pallas_call(
        kernel,
        out_shape=(
            jax.ShapeDtypeStruct(query_rows.shape, low),
            jax.ShapeDtypeStruct(key_rows.shape, low),
            jax.ShapeDtypeStruct(saved_value_rows.shape, low),
        ),
        in_specs=[anywhere] * 4,
        out_specs=(anywhere,) * 3,
        scratch_shapes=[
            pltpu.VMEM((2 * W, HEAD_SIZE), low),
            pltpu.VMEM((2 * W, HEAD_SIZE), low),
            pltpu.VMEM((2 * W // CHUNK, HEAD_SIZE, CHUNK), low),
            pltpu.VMEM((2, W, HEAD_SIZE), low),
            pltpu.VMEM((2, W, HEAD_SIZE), low),
            pltpu.VMEM((2 * W, HEAD_SIZE), wide),
            pltpu.VMEM((2 * W, HEAD_SIZE), wide),
            pltpu.VMEM((2, W, HEAD_SIZE), low),
            pltpu.VMEM((2, W, HEAD_SIZE), low),
            pltpu.VMEM((2, W, HEAD_SIZE), low),
            pltpu.VMEM((2, W, HEAD_SIZE), low),
            pltpu.VMEM((CHUNKS, CHUNK, QUERIES), wide),
            pltpu.VMEM((CHUNKS, CHUNK, QUERIES), wide),
            dma((6, LINE)),
            dma((6, BLOCKS)),
            dma((2,)),
            dma((2,)),
            dma((2, BLOCKS)),
            dma((2, LINE)),
            dma((2, STEPS)),
            dma((2, STEPS)),
            dma((2, BLOCKS)),
            dma((2, LINE)),
        ],
        compiler_params=pltpu.CompilerParams(collective_id=0, has_side_effects=True),
        name="attention_backward",
    )(query_rows, key_rows, saved_value_rows, out_grad)


def solution(mesh):
    rows_split = P(("seq", "head"), None)
    return jax.shard_map(
        on_device,
        mesh=mesh,
        in_specs=(rows_split,) * 4,
        out_specs=(rows_split,) * 3,
        check_vma=False,
    )
```

```python
import jax
import jax.numpy as jnp
from jax import lax
from jax.experimental import pallas as pl
from jax.experimental.pallas import tpu as pltpu
from jax.sharding import PartitionSpec as P

HEAD_SIZE = 128
W = 1024
BLOCKS = 8
BLOCK = W // BLOCKS
LINE = 8
DEPTH = 8
QUERIES = 256
STEPS = W // QUERIES
CHUNK = 256
CHUNKS = (W + QUERIES) // CHUNK
MESH = pl.DeviceIdType.MESH

score_scale = 168.0 ** (-0.5)
masked_value = -1e30
contract_last = (((1,), (1,)), ((), ()))

HOMES = (1, 7, 2, 6, 3, 5, 4)
OWNERS = ((0, 1), (1, 1), (0, 3), (1, 3), (0, 2), (1, 2), (1, 0))
KINDS = K, V, Q0, G0, Q1, G1 = range(6)


def kernel(
    query_in,
    key_in,
    value_in,
    grad_in,
    query_out,
    key_out,
    value_out,
    keys,
    values,
    keys_t,
    queries,
    grads,
    key_sum,
    value_sum,
    query_stage,
    back_stage,
    back_landing,
    own_stage,
    score_buf,
    prob_buf,
    in_send,
    in_recv,
    halo_send,
    halo_recv,
    query_send,
    query_recv,
    back_send,
    back_recv,
    own_send,
    own_recv,
    answer_sem,
    chain_sem,
    seam_sem,
):
    seq = lax.axis_index("seq")
    head = lax.axis_index("head")
    core = seq % 2
    z = seq // 2 % DEPTH
    y_lo = seq // (2 * DEPTH) % 2
    x = seq // (4 * DEPTH)
    y = head * 2 + y_lo
    mine = core * 4 + head
    alone = core == y_lo
    span = (x * 2 + core) * DEPTH + z
    span_count = lax.axis_size("seq") // 2
    first, last = span == 0, span == span_count - 1
    below, above = z > 0, z < DEPTH - 1

    def chip(other_y, other_core):
        other = (x * 2 + other_y % 2) * (2 * DEPTH) + z * 2 + other_core
        return {"seq": other, "head": other_y // 2}

    def span_home(other):
        place = (other // (2 * DEPTH) * 2 + y_lo) * (2 * DEPTH) + other % DEPTH * 2
        return {"seq": place + other // DEPTH % 2, "head": head}

    def owner(step):
        block_core, place = (core + step[0]) % 2, (head + step[1]) % 4
        return block_core * 4 + place, chip(place * 2 + core, block_core)

    homes = [((y + step) % LINE, chip((y + step) % LINE, y_lo)) for step in HOMES]
    owners = [owner(step) for step in OWNERS]
    near_home = (y, chip(y, y_lo))
    near_owner = owner((0, 0))
    following = span_home((span + 1) % span_count)
    preceding = span_home((span + span_count - 1) % span_count)

    def rows(block, size=BLOCK):
        return pl.ds(pl.multiple_of(block * size, size), size)

    def columns(index):
        return pl.ds(pl.multiple_of(index * HEAD_SIZE, HEAD_SIZE), HEAD_SIZE)

    def source(kind, home):
        if kind == K:
            return key_in.at[:, columns(home)]
        if kind == V:
            return value_in.at[:, columns(home)]
        array = query_in if kind in (Q0, Q1) else grad_in
        return array.at[:, columns(2 * home + (1 if kind in (Q1, G1) else 0))]

    def landing(kind, block):
        if kind == K:
            return keys.at[rows(BLOCKS + block)]
        if kind == V:
            return values.at[rows(BLOCKS + block)]
        array = queries if kind in (Q0, Q1) else grads
        return array.at[1 if kind in (Q1, G1) else 0, rows(block)]

    def local_in(kind):
        return pltpu.make_async_copy(source(kind, y), landing(kind, mine), in_recv.at[kind, mine])

    def remote_in(kind, home, device, block):
        return pltpu.make_async_remote_copy(
            src_ref=source(kind, home),
            dst_ref=landing(kind, block),
            send_sem=in_send.at[kind, home],
            recv_sem=in_recv.at[kind, block],
            device_id=device,
            device_id_type=MESH,
        )

    def wait_in(kind):
        for block, device in owners + [near_owner]:
            remote_in(kind, y, device, block).wait_recv()

    @pl.when(alone)
    def _():
        for kind in KINDS:
            local_in(kind).start()

    barrier = pltpu.get_barrier_semaphore()

    def greet(device):
        pl.semaphore_signal(barrier, inc=1, device_id=device, device_id_type=MESH)

    for _, device in homes:
        greet(device)
    for place in range(4):
        greet(chip(place * 2 + core, 1 - y_lo))

    foot = (z == 0) & (core == 1) & (x < span_count // (2 * DEPTH) - 1)

    @pl.when(jnp.logical_not(alone))
    def _():
        greet(near_home[1])

    @pl.when(above)
    def _():
        greet(following)

    @pl.when((z == 0) & (core == 0) & (x > 0))
    def _():
        greet(span_home(span - DEPTH))

    heard = len(homes) + 4 + jnp.where(alone, 0, 1) + jnp.where(below | foot, 1, 0)
    pl.semaphore_wait(barrier, heard)

    @pl.when(below)
    def _():
        pl.semaphore_signal(answer_sem, inc=1, device_id=preceding, device_id_type=MESH)

    for kind in KINDS:
        for home, device in homes:
            remote_in(kind, home, device, mine).start()

        @pl.when(jnp.logical_not(alone))
        def _():
            remote_in(kind, *near_home, mine).start()

    key_sum[...] = jnp.zeros_like(key_sum)
    value_sum[...] = jnp.zeros_like(value_sum)

    @pl.when(first)
    def _():
        keys[0:W, :] = jnp.zeros((W, HEAD_SIZE), jnp.bfloat16)
        values[0:W, :] = jnp.zeros((W, HEAD_SIZE), jnp.bfloat16)

    @pl.when(last)
    def _():
        back_landing[...] = jnp.zeros_like(back_landing)

    @pl.when(above)
    def _():
        pl.semaphore_wait(answer_sem, 1)

    @pl.when(below)
    def _():
        pl.semaphore_wait(chain_sem, 1)

    @pl.when(above)
    def _():
        pl.semaphore_signal(chain_sem, inc=1, device_id=following, device_id_type=MESH)

    @pl.when(jnp.logical_not(above | last))
    def _():
        pl.semaphore_signal(seam_sem, inc=1, device_id=following, device_id_type=MESH)

    def halo(which):
        array = keys if which == 0 else values
        return pltpu.make_async_remote_copy(
            src_ref=array.at[pl.ds(W, W)],
            dst_ref=array.at[pl.ds(0, W)],
            send_sem=halo_send.at[which],
            recv_sem=halo_recv.at[which],
            device_id=following,
            device_id_type=MESH,
        )

    wait_in(K)
    @pl.when(jnp.logical_not(last))
    def _():
        halo(0).start()

    wait_in(V)
    @pl.when(jnp.logical_not(last))
    def _():
        halo(1).start()

    @pl.when(jnp.logical_not(first))
    def _():
        halo(0).wait_recv()


    @pl.loop(0, 2 * W // CHUNK)
    def _(chunk):
        keys_t[chunk] = keys[rows(chunk, CHUNK), :].T

    @pl.when(jnp.logical_not(first))
    def _():
        halo(1).wait_recv()


    key_row = lax.broadcasted_iota(jnp.int32, (CHUNK, QUERIES), 0)
    query_row = lax.broadcasted_iota(jnp.int32, (CHUNK, QUERIES), 1)

    def compute(q_head, step):
        query = queries[q_head, rows(step, QUERIES), :]
        grad = grads[q_head, rows(step, QUERIES), :]
        peak = None
        for part in range(CHUNKS):
            scores = (
                lax.dot_general(
                    keys[rows(step + part, CHUNK), :],
                    query,
                    contract_last,
                    preferred_element_type=jnp.float32,
                )
                * score_scale
            )
            if part < CHUNKS - 1:
                absent = (span == 0) & (step + part < W // CHUNK)
                scores = scores + jnp.where(absent, masked_value, 0.0)
            if part == 0:
                scores = jnp.where(key_row > query_row, scores, masked_value)
            if part == CHUNKS - 1:
                scores = jnp.where(key_row <= query_row, scores, masked_value)
            score_buf[part] = scores
            top = jnp.max(scores, axis=0, keepdims=True)
            peak = top if peak is None else jnp.maximum(peak, top)
        total = jnp.zeros((1, QUERIES), jnp.float32)
        delta = jnp.zeros((1, QUERIES), jnp.float32)
        for part in range(CHUNKS):
            weights = jnp.exp(score_buf[part] - peak)
            prob_grad = lax.dot_general(
                values[rows(step + part, CHUNK), :],
                grad,
                contract_last,
                preferred_element_type=jnp.float32,
            )
            score_buf[part] = weights
            prob_buf[part] = prob_grad
            total = total + jnp.sum(weights, axis=0, keepdims=True)
            delta = delta + jnp.sum(weights * prob_grad, axis=0, keepdims=True)
        inverse = 1.0 / total
        delta = delta * inverse
        query_grad = jnp.zeros((HEAD_SIZE, QUERIES), jnp.float32)
        for part in range(CHUNKS):
            attention = score_buf[part] * inverse
            score_grad = (score_scale * attention * (prob_buf[part] - delta)).astype(jnp.bfloat16)
            at = rows(step + part, CHUNK)
            value_sum[at, :] += jnp.dot(
                attention.astype(jnp.bfloat16), grad, preferred_element_type=jnp.float32
            )
            key_sum[at, :] += jnp.dot(score_grad, query, preferred_element_type=jnp.float32)
            query_grad = query_grad + jnp.dot(
                keys_t[step + part], score_grad, preferred_element_type=jnp.float32
            )
        query_stage[q_head, rows(step, QUERIES), :] = query_grad.T.astype(jnp.bfloat16)

    def query_local(q_head):
        return pltpu.make_async_copy(
            query_stage.at[q_head, rows(mine)],
            query_out.at[:, columns(2 * y + q_head)],
            query_recv.at[q_head, y],
        )

    def query_remote(q_head, block, device, home):
        return pltpu.make_async_remote_copy(
            src_ref=query_stage.at[q_head, rows(block)],
            dst_ref=query_out.at[:, columns(2 * home + q_head)],
            send_sem=query_send.at[q_head, block],
            recv_sem=query_recv.at[q_head, home],
            device_id=device,
            device_id_type=MESH,
        )

    def send_rows(step, local, remote):
        for block in (2 * step, 2 * step + 1):
            device = chip(block % 4 * 2 + core, block // 4)
            here = alone & (block == mine)

            @pl.when(here)
            def _():
                local()

            @pl.when(jnp.logical_not(here))
            def _():
                remote(block, device)

    def send_query(q_head, step):
        send_rows(
            step,
            lambda: query_local(q_head).start(),
            lambda block, device: query_remote(q_head, block, device, y).start(),
        )

    def back(which, step):
        return pltpu.make_async_remote_copy(
            src_ref=back_stage.at[which, rows(step, QUERIES)],
            dst_ref=back_landing.at[which, rows(step, QUERIES)],
            send_sem=back_send.at[which, step],
            recv_sem=back_recv.at[which, step],
            device_id=preceding,
            device_id_type=MESH,
        )

    wait_in(Q0)
    wait_in(G0)

    @pl.loop(0, STEPS)
    def _(step):
        compute(0, step)
        send_query(0, step)

    wait_in(Q1)
    wait_in(G1)

    @pl.when(jnp.logical_not(below | first))
    def _():
        pl.semaphore_wait(seam_sem, 1)

    @pl.loop(0, STEPS)
    def _(step):
        compute(1, step)
        at = rows(step, QUERIES)
        back_stage[0, at, :] = key_sum[at, :].astype(jnp.bfloat16)
        back_stage[1, at, :] = value_sum[at, :].astype(jnp.bfloat16)

        @pl.when(jnp.logical_not(first))
        def _():
            back(0, step).start()
            back(1, step).start()

        send_query(1, step)

    def own_out(which):
        return key_out if which == 0 else value_out

    def own_local(which):
        return pltpu.make_async_copy(
            own_stage.at[which, rows(mine)],
            own_out(which).at[:, columns(y)],
            own_recv.at[which, y],
        )

    def own_remote(which, block, device, home):
        return pltpu.make_async_remote_copy(
            src_ref=own_stage.at[which, rows(block)],
            dst_ref=own_out(which).at[:, columns(home)],
            send_sem=own_send.at[which, block],
            recv_sem=own_recv.at[which, home],
            device_id=device,
            device_id_type=MESH,
        )

    @pl.loop(0, STEPS)
    def _(step):
        at = rows(step, QUERIES)
        own = rows(STEPS + step, QUERIES)

        @pl.when(jnp.logical_not(last))
        def _():
            back(0, step).wait_recv()
            back(1, step).wait_recv()

        for which, sums in ((0, key_sum), (1, value_sum)):
            own_stage[which, at, :] = (
                sums[own, :] + back_landing[which, at, :].astype(jnp.float32)
            ).astype(jnp.bfloat16)

        def local():
            own_local(0).start()
            own_local(1).start()

        def remote(block, device):
            own_remote(0, block, device, y).start()
            own_remote(1, block, device, y).start()

        send_rows(step, local, remote)

    @pl.when(jnp.logical_not(alone))
    def _():
        for kind in KINDS:
            remote_in(kind, *near_home, mine).wait_send()
        for which in (0, 1):
            query_remote(which, *near_owner, y).wait_send()
            own_remote(which, *near_owner, y).wait_send()

    for kind in KINDS:
        for home, device in homes:
            remote_in(kind, home, device, mine).wait_send()
    @pl.when(jnp.logical_not(last))
    def _():
        halo(0).wait_send()
        halo(1).wait_send()

    @pl.when(jnp.logical_not(first))
    def _():
        for step in range(STEPS):
            back(0, step).wait_send()
            back(1, step).wait_send()

    for which in (0, 1):
        for block, device in owners:
            query_remote(which, block, device, y).wait_send()
            own_remote(which, block, device, y).wait_send()
        for home, device in homes + [near_home]:
            query_remote(which, mine, device, home).wait_recv()
            own_remote(which, mine, device, home).wait_recv()


def store(query_from, key_from, value_from, query_to, key_to, value_to, done):
    pairs = ((query_from, query_to), (key_from, key_to), (value_from, value_to))
    copies = [
        pltpu.make_async_copy(source, target, done.at[index])
        for index, (source, target) in enumerate(pairs)
    ]
    for copy in copies:
        copy.start()
    for copy in copies:
        copy.wait()


def on_device(query_rows, key_rows, saved_value_rows, out_grad):
    dma = pltpu.SemaphoreType.DMA
    low, wide = jnp.bfloat16, jnp.float32
    anywhere = pl.BlockSpec(memory_space=pl.ANY)
    in_hbm = pl.BlockSpec(memory_space=pltpu.HBM)
    results = pl.pallas_call(
        kernel,
        out_shape=(
            pltpu.VMEM(query_rows.shape, low),
            pltpu.VMEM(key_rows.shape, low),
            pltpu.VMEM(saved_value_rows.shape, low),
        ),
        in_specs=[in_hbm] * 4,
        out_specs=(anywhere,) * 3,
        scratch_shapes=[
            pltpu.VMEM((2 * W, HEAD_SIZE), low),
            pltpu.VMEM((2 * W, HEAD_SIZE), low),
            pltpu.VMEM((2 * W // CHUNK, HEAD_SIZE, CHUNK), low),
            pltpu.VMEM((2, W, HEAD_SIZE), low),
            pltpu.VMEM((2, W, HEAD_SIZE), low),
            pltpu.VMEM((2 * W, HEAD_SIZE), wide),
            pltpu.VMEM((2 * W, HEAD_SIZE), wide),
            pltpu.VMEM((2, W, HEAD_SIZE), low),
            pltpu.VMEM((2, W, HEAD_SIZE), low),
            pltpu.VMEM((2, W, HEAD_SIZE), low),
            pltpu.VMEM((2, W, HEAD_SIZE), low),
            pltpu.VMEM((CHUNKS, CHUNK, QUERIES), wide),
            pltpu.VMEM((CHUNKS, CHUNK, QUERIES), wide),
            dma((6, LINE)),
            dma((6, BLOCKS)),
            dma((2,)),
            dma((2,)),
            dma((2, BLOCKS)),
            dma((2, LINE)),
            dma((2, STEPS)),
            dma((2, STEPS)),
            dma((2, BLOCKS)),
            dma((2, LINE)),
            pltpu.SemaphoreType.REGULAR,
            pltpu.SemaphoreType.REGULAR,
            pltpu.SemaphoreType.REGULAR,
        ],
        compiler_params=pltpu.CompilerParams(
            collective_id=0, has_side_effects=True
        ),
        name="attention_backward",
    )(query_rows, key_rows, saved_value_rows, out_grad)
    in_vmem = pl.BlockSpec(memory_space=pltpu.VMEM)
    return pl.pallas_call(
        store,
        out_shape=tuple(jax.ShapeDtypeStruct(result.shape, low) for result in results),
        in_specs=[in_vmem] * 3,
        out_specs=(in_hbm,) * 3,
        scratch_shapes=[dma((3,))],
        compiler_params=pltpu.CompilerParams(vmem_limit_bytes=4 * 2**20),
        name="store",
    )(*results)


def solution(mesh):
    rows_split = P(("seq", "head"), None)
    return jax.shard_map(
        on_device,
        mesh=mesh,
        in_specs=(rows_split,) * 4,
        out_specs=(rows_split,) * 3,
        check_vma=False,
    )
```

```python
import jax
import jax.numpy as jnp
from jax import lax
from jax.experimental import pallas as pl
from jax.experimental.pallas import tpu as pltpu
from jax.sharding import PartitionSpec as P

HEAD_SIZE = 128
W = 1024
BLOCKS = 8
BLOCK = W // BLOCKS
LINE = 8
DEPTH = 8
QUERIES = 256
STEPS = W // QUERIES
CHUNK = 256
CHUNKS = (W + QUERIES) // CHUNK
MESH = pl.DeviceIdType.MESH

score_scale = 168.0 ** (-0.5)
masked_value = -1e30
contract_last = (((1,), (1,)), ((), ()))

HOMES = (3, 5, 1, 7, 4, 2, 6)
OWNERS = ((0, 1), (1, 1), (0, 3), (1, 3), (0, 2), (1, 2), (1, 0))
KINDS = K, V, Q0, G0, Q1, G1 = range(6)


def kernel(
    query_in,
    key_in,
    value_in,
    grad_in,
    query_out,
    key_out,
    value_out,
    keys,
    values,
    keys_t,
    queries,
    grads,
    key_sum,
    value_sum,
    query_stage,
    back_stage,
    back_landing,
    own_stage,
    score_buf,
    prob_buf,
    in_send,
    in_recv,
    halo_send,
    halo_recv,
    query_send,
    query_recv,
    back_send,
    back_recv,
    own_send,
    own_recv,
    answer_sem,
    chain_sem,
    seam_sem,
    foot_sem,
):
    seq = lax.axis_index("seq")
    head = lax.axis_index("head")
    core = seq % 2
    z = seq // 2 % DEPTH
    y_lo = seq // (2 * DEPTH) % 2
    x = seq // (4 * DEPTH)
    y = head * 2 + y_lo
    mine = core * 4 + head
    alone = core == y_lo
    span = (x * 2 + core) * DEPTH + z
    span_count = lax.axis_size("seq") // 2
    first, last = span == 0, span == span_count - 1
    below, above = z > 0, z < DEPTH - 1

    def chip(other_y, other_core):
        other = (x * 2 + other_y % 2) * (2 * DEPTH) + z * 2 + other_core
        return {"seq": other, "head": other_y // 2}

    def span_home(other):
        place = (other // (2 * DEPTH) * 2 + y_lo) * (2 * DEPTH) + other % DEPTH * 2
        return {"seq": place + other // DEPTH % 2, "head": head}

    def owner(step):
        block_core, place = (core + step[0]) % 2, (head + step[1]) % 4
        return block_core * 4 + place, chip(place * 2 + core, block_core)

    homes = [((y + step) % LINE, chip((y + step) % LINE, y_lo)) for step in HOMES]
    owners = [owner(step) for step in OWNERS]
    near_home = (y, chip(y, y_lo))
    near_owner = owner((0, 0))
    following = span_home((span + 1) % span_count)
    preceding = span_home((span + span_count - 1) % span_count)

    def rows(block, size=BLOCK):
        return pl.ds(pl.multiple_of(block * size, size), size)

    def columns(index):
        return pl.ds(pl.multiple_of(index * HEAD_SIZE, HEAD_SIZE), HEAD_SIZE)

    def source(kind, home):
        if kind == K:
            return key_in.at[:, columns(home)]
        if kind == V:
            return value_in.at[:, columns(home)]
        array = query_in if kind in (Q0, Q1) else grad_in
        return array.at[:, columns(2 * home + (1 if kind in (Q1, G1) else 0))]

    def landing(kind, block):
        if kind == K:
            return keys.at[rows(BLOCKS + block)]
        if kind == V:
            return values.at[rows(BLOCKS + block)]
        array = queries if kind in (Q0, Q1) else grads
        return array.at[1 if kind in (Q1, G1) else 0, rows(block)]

    def local_in(kind):
        return pltpu.make_async_copy(source(kind, y), landing(kind, mine), in_recv.at[kind, mine])

    def remote_in(kind, home, device, block):
        return pltpu.make_async_remote_copy(
            src_ref=source(kind, home),
            dst_ref=landing(kind, block),
            send_sem=in_send.at[kind, home],
            recv_sem=in_recv.at[kind, block],
            device_id=device,
            device_id_type=MESH,
        )

    def wait_in(kind):
        for block, device in owners + [near_owner]:
            remote_in(kind, y, device, block).wait_recv()

    @pl.when(alone)
    def _():
        for kind in KINDS:
            local_in(kind).start()

    barrier = pltpu.get_barrier_semaphore()

    def greet(device):
        pl.semaphore_signal(barrier, inc=1, device_id=device, device_id_type=MESH)

    for _, device in homes:
        greet(device)
    for place in range(4):
        greet(chip(place * 2 + core, 1 - y_lo))

    foot = (z == 0) & (core == 1) & (x < span_count // (2 * DEPTH) - 1)
    next_foot = (z == 0) & (core == 0) & (x > 0)

    @pl.when(jnp.logical_not(alone))
    def _():
        greet(near_home[1])

    @pl.when(above)
    def _():
        greet(following)

    @pl.when(foot)
    def _():
        greet(span_home(span + DEPTH))

    heard = len(homes) + 4 + jnp.where(alone, 0, 1) + jnp.where(below | next_foot, 1, 0)
    pl.semaphore_wait(barrier, heard)

    @pl.when(below)
    def _():
        pl.semaphore_signal(answer_sem, inc=1, device_id=preceding, device_id_type=MESH)

    @pl.when(next_foot)
    def _():
        device = span_home(span - DEPTH)
        pl.semaphore_signal(foot_sem, inc=1, device_id=device, device_id_type=MESH)

    for kind in KINDS:
        for home, device in homes:
            remote_in(kind, home, device, mine).start()

        @pl.when(jnp.logical_not(alone))
        def _():
            remote_in(kind, *near_home, mine).start()

    key_sum[...] = jnp.zeros_like(key_sum)
    value_sum[...] = jnp.zeros_like(value_sum)

    @pl.when(first)
    def _():
        keys[0:W, :] = jnp.zeros((W, HEAD_SIZE), jnp.bfloat16)
        values[0:W, :] = jnp.zeros((W, HEAD_SIZE), jnp.bfloat16)

    @pl.when(last)
    def _():
        back_landing[...] = jnp.zeros_like(back_landing)

    @pl.when(above)
    def _():
        pl.semaphore_wait(answer_sem, 1)

    @pl.when(below)
    def _():
        pl.semaphore_wait(chain_sem, 1)

    @pl.when(foot)
    def _():
        pl.semaphore_wait(foot_sem, 1)

    @pl.when(above)
    def _():
        pl.semaphore_signal(chain_sem, inc=1, device_id=following, device_id_type=MESH)

    @pl.when(jnp.logical_not(above | last))
    def _():
        pl.semaphore_signal(seam_sem, inc=1, device_id=following, device_id_type=MESH)

    def halo(which):
        array = keys if which == 0 else values
        return pltpu.make_async_remote_copy(
            src_ref=array.at[pl.ds(W, W)],
            dst_ref=array.at[pl.ds(0, W)],
            send_sem=halo_send.at[which],
            recv_sem=halo_recv.at[which],
            device_id=following,
            device_id_type=MESH,
        )

    wait_in(K)
    @pl.when(jnp.logical_not(last))
    def _():
        halo(0).start()

    wait_in(V)
    @pl.when(jnp.logical_not(last))
    def _():
        halo(1).start()

    @pl.when(jnp.logical_not(first))
    def _():
        halo(0).wait_recv()


    @pl.loop(0, 2 * W // CHUNK)
    def _(chunk):
        keys_t[chunk] = keys[rows(chunk, CHUNK), :].T

    @pl.when(jnp.logical_not(first))
    def _():
        halo(1).wait_recv()


    key_row = lax.broadcasted_iota(jnp.int32, (CHUNK, QUERIES), 0)
    query_row = lax.broadcasted_iota(jnp.int32, (CHUNK, QUERIES), 1)

    def compute(q_head, step):
        query = queries[q_head, rows(step, QUERIES), :]
        grad = grads[q_head, rows(step, QUERIES), :]
        peak = None
        for part in range(CHUNKS):
            scores = (
                lax.dot_general(
                    keys[rows(step + part, CHUNK), :],
                    query,
                    contract_last,
                    preferred_element_type=jnp.float32,
                )
                * score_scale
            )
            if part < CHUNKS - 1:
                absent = (span == 0) & (step + part < W // CHUNK)
                scores = scores + jnp.where(absent, masked_value, 0.0)
            if part == 0:
                scores = jnp.where(key_row > query_row, scores, masked_value)
            if part == CHUNKS - 1:
                scores = jnp.where(key_row <= query_row, scores, masked_value)
            score_buf[part] = scores
            top = jnp.max(scores, axis=0, keepdims=True)
            peak = top if peak is None else jnp.maximum(peak, top)
        total = jnp.zeros((1, QUERIES), jnp.float32)
        delta = jnp.zeros((1, QUERIES), jnp.float32)
        for part in range(CHUNKS):
            weights = jnp.exp(score_buf[part] - peak)
            prob_grad = lax.dot_general(
                values[rows(step + part, CHUNK), :],
                grad,
                contract_last,
                preferred_element_type=jnp.float32,
            )
            score_buf[part] = weights
            prob_buf[part] = prob_grad
            total = total + jnp.sum(weights, axis=0, keepdims=True)
            delta = delta + jnp.sum(weights * prob_grad, axis=0, keepdims=True)
        inverse = 1.0 / total
        delta = delta * inverse
        query_grad = jnp.zeros((HEAD_SIZE, QUERIES), jnp.float32)
        for part in range(CHUNKS):
            attention = score_buf[part] * inverse
            score_grad = (score_scale * attention * (prob_buf[part] - delta)).astype(jnp.bfloat16)
            at = rows(step + part, CHUNK)
            value_sum[at, :] += jnp.dot(
                attention.astype(jnp.bfloat16), grad, preferred_element_type=jnp.float32
            )
            key_sum[at, :] += jnp.dot(score_grad, query, preferred_element_type=jnp.float32)
            query_grad = query_grad + jnp.dot(
                keys_t[step + part], score_grad, preferred_element_type=jnp.float32
            )
        query_stage[q_head, rows(step, QUERIES), :] = query_grad.T.astype(jnp.bfloat16)

    def query_local(q_head):
        return pltpu.make_async_copy(
            query_stage.at[q_head, rows(mine)],
            query_out.at[:, columns(2 * y + q_head)],
            query_recv.at[q_head, y],
        )

    def query_remote(q_head, block, device, home):
        return pltpu.make_async_remote_copy(
            src_ref=query_stage.at[q_head, rows(block)],
            dst_ref=query_out.at[:, columns(2 * home + q_head)],
            send_sem=query_send.at[q_head, block],
            recv_sem=query_recv.at[q_head, home],
            device_id=device,
            device_id_type=MESH,
        )

    def send_rows(step, local, remote):
        for block in (2 * step, 2 * step + 1):
            device = chip(block % 4 * 2 + core, block // 4)
            here = alone & (block == mine)

            @pl.when(here)
            def _():
                local()

            @pl.when(jnp.logical_not(here))
            def _():
                remote(block, device)

    def send_query(q_head, step):
        send_rows(
            step,
            lambda: query_local(q_head).start(),
            lambda block, device: query_remote(q_head, block, device, y).start(),
        )

    def back(which, step):
        return pltpu.make_async_remote_copy(
            src_ref=back_stage.at[which, rows(step, QUERIES)],
            dst_ref=back_landing.at[which, rows(step, QUERIES)],
            send_sem=back_send.at[which, step],
            recv_sem=back_recv.at[which, step],
            device_id=preceding,
            device_id_type=MESH,
        )

    wait_in(Q0)
    wait_in(G0)

    @pl.loop(0, STEPS)
    def _(step):
        compute(0, step)

        @pl.when(step < 2)
        def _():
            send_query(0, step)

    wait_in(Q1)
    wait_in(G1)
    for step in (2, 3):
        send_query(0, step)

    @pl.when(jnp.logical_not(below | first))
    def _():
        pl.semaphore_wait(seam_sem, 1)

    @pl.loop(0, STEPS)
    def _(step):
        compute(1, step)
        at = rows(step, QUERIES)
        back_stage[0, at, :] = key_sum[at, :].astype(jnp.bfloat16)
        back_stage[1, at, :] = value_sum[at, :].astype(jnp.bfloat16)

        @pl.when(jnp.logical_not(first))
        def _():
            back(0, step).start()
            back(1, step).start()

        send_query(1, step)

    def own_out(which):
        return key_out if which == 0 else value_out

    def own_local(which):
        return pltpu.make_async_copy(
            own_stage.at[which, rows(mine)],
            own_out(which).at[:, columns(y)],
            own_recv.at[which, y],
        )

    def own_remote(which, block, device, home):
        return pltpu.make_async_remote_copy(
            src_ref=own_stage.at[which, rows(block)],
            dst_ref=own_out(which).at[:, columns(home)],
            send_sem=own_send.at[which, block],
            recv_sem=own_recv.at[which, home],
            device_id=device,
            device_id_type=MESH,
        )

    @pl.loop(0, STEPS)
    def _(step):
        at = rows(step, QUERIES)
        own = rows(STEPS + step, QUERIES)

        @pl.when(jnp.logical_not(last))
        def _():
            back(0, step).wait_recv()
            back(1, step).wait_recv()

        for which, sums in ((0, key_sum), (1, value_sum)):
            own_stage[which, at, :] = (
                sums[own, :] + back_landing[which, at, :].astype(jnp.float32)
            ).astype(jnp.bfloat16)

        def local():
            own_local(0).start()
            own_local(1).start()

        def remote(block, device):
            own_remote(0, block, device, y).start()
            own_remote(1, block, device, y).start()

        send_rows(step, local, remote)

    @pl.when(jnp.logical_not(alone))
    def _():
        for kind in KINDS:
            remote_in(kind, *near_home, mine).wait_send()
        for which in (0, 1):
            query_remote(which, *near_owner, y).wait_send()
            own_remote(which, *near_owner, y).wait_send()

    for kind in KINDS:
        for home, device in homes:
            remote_in(kind, home, device, mine).wait_send()
    @pl.when(jnp.logical_not(last))
    def _():
        halo(0).wait_send()
        halo(1).wait_send()

    @pl.when(jnp.logical_not(first))
    def _():
        for step in range(STEPS):
            back(0, step).wait_send()
            back(1, step).wait_send()

    for which in (0, 1):
        for block, device in owners:
            query_remote(which, block, device, y).wait_send()
            own_remote(which, block, device, y).wait_send()
        for home, device in homes + [near_home]:
            query_remote(which, mine, device, home).wait_recv()
            own_remote(which, mine, device, home).wait_recv()


def store(query_from, key_from, value_from, query_to, key_to, value_to, done):
    pairs = ((query_from, query_to), (key_from, key_to), (value_from, value_to))
    copies = [
        pltpu.make_async_copy(source, target, done.at[index])
        for index, (source, target) in enumerate(pairs)
    ]
    for copy in copies:
        copy.start()
    for copy in copies:
        copy.wait()


def on_device(query_rows, key_rows, saved_value_rows, out_grad):
    dma = pltpu.SemaphoreType.DMA
    low, wide = jnp.bfloat16, jnp.float32
    anywhere = pl.BlockSpec(memory_space=pl.ANY)
    in_hbm = pl.BlockSpec(memory_space=pltpu.HBM)
    results = pl.pallas_call(
        kernel,
        out_shape=(
            pltpu.VMEM(query_rows.shape, low),
            pltpu.VMEM(key_rows.shape, low),
            pltpu.VMEM(saved_value_rows.shape, low),
        ),
        in_specs=[in_hbm] * 4,
        out_specs=(anywhere,) * 3,
        scratch_shapes=[
            pltpu.VMEM((2 * W, HEAD_SIZE), low),
            pltpu.VMEM((2 * W, HEAD_SIZE), low),
            pltpu.VMEM((2 * W // CHUNK, HEAD_SIZE, CHUNK), low),
            pltpu.VMEM((2, W, HEAD_SIZE), low),
            pltpu.VMEM((2, W, HEAD_SIZE), low),
            pltpu.VMEM((2 * W, HEAD_SIZE), wide),
            pltpu.VMEM((2 * W, HEAD_SIZE), wide),
            pltpu.VMEM((2, W, HEAD_SIZE), low),
            pltpu.VMEM((2, W, HEAD_SIZE), low),
            pltpu.VMEM((2, W, HEAD_SIZE), low),
            pltpu.VMEM((2, W, HEAD_SIZE), low),
            pltpu.VMEM((CHUNKS, CHUNK, QUERIES), wide),
            pltpu.VMEM((CHUNKS, CHUNK, QUERIES), wide),
            dma((6, LINE)),
            dma((6, BLOCKS)),
            dma((2,)),
            dma((2,)),
            dma((2, BLOCKS)),
            dma((2, LINE)),
            dma((2, STEPS)),
            dma((2, STEPS)),
            dma((2, BLOCKS)),
            dma((2, LINE)),
            pltpu.SemaphoreType.REGULAR,
            pltpu.SemaphoreType.REGULAR,
            pltpu.SemaphoreType.REGULAR,
            pltpu.SemaphoreType.REGULAR,
        ],
        compiler_params=pltpu.CompilerParams(
            collective_id=0, has_side_effects=True
        ),
        name="attention_backward",
    )(query_rows, key_rows, saved_value_rows, out_grad)
    in_vmem = pl.BlockSpec(memory_space=pltpu.VMEM)
    return pl.pallas_call(
        store,
        out_shape=tuple(jax.ShapeDtypeStruct(result.shape, low) for result in results),
        in_specs=[in_vmem] * 3,
        out_specs=(in_hbm,) * 3,
        scratch_shapes=[dma((3,))],
        compiler_params=pltpu.CompilerParams(vmem_limit_bytes=4 * 2**20),
        name="store",
    )(*results)


def solution(mesh):
    rows_split = P(("seq", "head"), None)
    return jax.shard_map(
        on_device,
        mesh=mesh,
        in_specs=(rows_split,) * 4,
        out_specs=(rows_split,) * 3,
        check_vma=False,
    )
```

```python
import math

import jax
import jax.numpy as jnp
from jax import lax
from jax.experimental import pallas as pl
from jax.experimental.pallas import tpu as pltpu
from jax.sharding import PartitionSpec as P

HEAD_SIZE = 128
W = 1024
BLOCKS = 8
BLOCK = W // BLOCKS
LINE = 8
DEPTH = 8
QUERIES = 256
STEPS = W // QUERIES
CHUNK = 256
CHUNKS = (W + QUERIES) // CHUNK
MESH = pl.DeviceIdType.MESH

score_scale = 168.0 ** (-0.5)
binary_scale = score_scale * math.log2(math.e)
masked_value = -1e30
contract_last = (((1,), (1,)), ((), ()))

HOMES = (3, 5, 4, 1, 7, 2, 6)
OWNERS = ((0, 1), (1, 1), (0, 3), (1, 3), (0, 2), (1, 2), (1, 0))
KINDS = K, V, Q0, G0, Q1, G1 = range(6)


def kernel(
    query_in,
    key_in,
    value_in,
    grad_in,
    query_out,
    key_out,
    value_out,
    keys,
    values,
    keys_t,
    queries,
    grads,
    key_sum,
    value_sum,
    query_stage,
    back_stage,
    back_landing,
    own_stage,
    score_buf,
    prob_buf,
    in_send,
    in_recv,
    halo_send,
    halo_recv,
    query_send,
    query_recv,
    back_send,
    back_recv,
    own_send,
    own_recv,
    answer_sem,
    chain_sem,
    seam_sem,
    foot_sem,
):
    seq = lax.axis_index("seq")
    head = lax.axis_index("head")
    core = seq % 2
    z = seq // 2 % DEPTH
    y_lo = seq // (2 * DEPTH) % 2
    x = seq // (4 * DEPTH)
    y = head * 2 + y_lo
    mine = core * 4 + head
    alone = core == y_lo
    span = (x * 2 + core) * DEPTH + z
    span_count = lax.axis_size("seq") // 2
    first, last = span == 0, span == span_count - 1
    below, above = z > 0, z < DEPTH - 1

    def chip(other_y, other_core):
        other = (x * 2 + other_y % 2) * (2 * DEPTH) + z * 2 + other_core
        return {"seq": other, "head": other_y // 2}

    def span_home(other):
        place = (other // (2 * DEPTH) * 2 + y_lo) * (2 * DEPTH) + other % DEPTH * 2
        return {"seq": place + other // DEPTH % 2, "head": head}

    def owner(step):
        block_core, place = (core + step[0]) % 2, (head + step[1]) % 4
        return block_core * 4 + place, chip(place * 2 + core, block_core)

    homes = [((y + step) % LINE, chip((y + step) % LINE, y_lo)) for step in HOMES]
    owners = [owner(step) for step in OWNERS]
    near_home = (y, chip(y, y_lo))
    near_owner = owner((0, 0))
    following = span_home((span + 1) % span_count)
    preceding = span_home((span + span_count - 1) % span_count)

    def rows(block, size=BLOCK):
        return pl.ds(pl.multiple_of(block * size, size), size)

    def columns(index):
        return pl.ds(pl.multiple_of(index * HEAD_SIZE, HEAD_SIZE), HEAD_SIZE)

    def source(kind, home):
        if kind == K:
            return key_in.at[:, columns(home)]
        if kind == V:
            return value_in.at[:, columns(home)]
        array = query_in if kind in (Q0, Q1) else grad_in
        return array.at[:, columns(2 * home + (1 if kind in (Q1, G1) else 0))]

    def landing(kind, block):
        if kind == K:
            return keys.at[rows(BLOCKS + block)]
        if kind == V:
            return values.at[rows(BLOCKS + block)]
        array = queries if kind in (Q0, Q1) else grads
        return array.at[1 if kind in (Q1, G1) else 0, rows(block)]

    def local_in(kind):
        return pltpu.make_async_copy(source(kind, y), landing(kind, mine), in_recv.at[kind, mine])

    def remote_in(kind, home, device, block):
        return pltpu.make_async_remote_copy(
            src_ref=source(kind, home),
            dst_ref=landing(kind, block),
            send_sem=in_send.at[kind, home],
            recv_sem=in_recv.at[kind, block],
            device_id=device,
            device_id_type=MESH,
        )

    def wait_in(kind):
        for block, device in owners + [near_owner]:
            remote_in(kind, y, device, block).wait_recv()

    @pl.when(alone)
    def _():
        for kind in KINDS:
            local_in(kind).start()

    barrier = pltpu.get_barrier_semaphore()

    def greet(device):
        pl.semaphore_signal(barrier, inc=1, device_id=device, device_id_type=MESH)

    for _, device in homes:
        greet(device)
    for place in range(4):
        greet(chip(place * 2 + core, 1 - y_lo))

    foot = (z == 0) & (core == 1) & (x < span_count // (2 * DEPTH) - 1)
    next_foot = (z == 0) & (core == 0) & (x > 0)

    @pl.when(jnp.logical_not(alone))
    def _():
        greet(near_home[1])

    @pl.when(above)
    def _():
        greet(following)

    @pl.when(foot)
    def _():
        greet(span_home(span + DEPTH))

    heard = len(homes) + 4 + jnp.where(alone, 0, 1) + jnp.where(below | next_foot, 1, 0)
    pl.semaphore_wait(barrier, heard)

    @pl.when(below)
    def _():
        pl.semaphore_signal(answer_sem, inc=1, device_id=preceding, device_id_type=MESH)

    @pl.when(next_foot)
    def _():
        device = span_home(span - DEPTH)
        pl.semaphore_signal(foot_sem, inc=1, device_id=device, device_id_type=MESH)

    for kind in KINDS:
        for home, device in homes:
            remote_in(kind, home, device, mine).start()

        @pl.when(jnp.logical_not(alone))
        def _():
            remote_in(kind, *near_home, mine).start()

    key_sum[...] = jnp.zeros_like(key_sum)
    value_sum[...] = jnp.zeros_like(value_sum)

    @pl.when(first)
    def _():
        keys[0:W, :] = jnp.zeros((W, HEAD_SIZE), jnp.bfloat16)
        values[0:W, :] = jnp.zeros((W, HEAD_SIZE), jnp.bfloat16)

    @pl.when(last)
    def _():
        back_landing[...] = jnp.zeros_like(back_landing)

    @pl.when(above)
    def _():
        pl.semaphore_wait(answer_sem, 1)

    @pl.when(below)
    def _():
        pl.semaphore_wait(chain_sem, 1)

    @pl.when(foot)
    def _():
        pl.semaphore_wait(foot_sem, 1)

    @pl.when(above)
    def _():
        pl.semaphore_signal(chain_sem, inc=1, device_id=following, device_id_type=MESH)

    @pl.when(jnp.logical_not(above | last))
    def _():
        pl.semaphore_signal(seam_sem, inc=1, device_id=following, device_id_type=MESH)

    def halo(which):
        array = keys if which == 0 else values
        return pltpu.make_async_remote_copy(
            src_ref=array.at[pl.ds(W, W)],
            dst_ref=array.at[pl.ds(0, W)],
            send_sem=halo_send.at[which],
            recv_sem=halo_recv.at[which],
            device_id=following,
            device_id_type=MESH,
        )

    wait_in(K)
    @pl.when(jnp.logical_not(last))
    def _():
        halo(0).start()

    wait_in(V)
    @pl.when(jnp.logical_not(last))
    def _():
        halo(1).start()

    @pl.when(jnp.logical_not(first))
    def _():
        halo(0).wait_recv()


    @pl.loop(0, 2 * W // CHUNK)
    def _(chunk):
        keys_t[chunk] = keys[rows(chunk, CHUNK), :].T

    @pl.when(jnp.logical_not(first))
    def _():
        halo(1).wait_recv()


    key_row = lax.broadcasted_iota(jnp.int32, (CHUNK, QUERIES), 0)
    query_row = lax.broadcasted_iota(jnp.int32, (CHUNK, QUERIES), 1)

    def compute(q_head, step):
        query = queries[q_head, rows(step, QUERIES), :]
        grad = grads[q_head, rows(step, QUERIES), :]
        peak = None
        for part in range(CHUNKS):
            scores = (
                lax.dot_general(
                    keys[rows(step + part, CHUNK), :],
                    query,
                    contract_last,
                    preferred_element_type=jnp.float32,
                )
                * binary_scale
            )
            if part < CHUNKS - 1:
                absent = (span == 0) & (step + part < W // CHUNK)
                scores = scores + jnp.where(absent, masked_value, 0.0)
            if part == 0:
                scores = jnp.where(key_row > query_row, scores, masked_value)
            if part == CHUNKS - 1:
                scores = jnp.where(key_row <= query_row, scores, masked_value)
            score_buf[part] = scores
            top = jnp.max(scores, axis=0, keepdims=True)
            peak = top if peak is None else jnp.maximum(peak, top)
        total = jnp.zeros((1, QUERIES), jnp.float32)
        delta = jnp.zeros((1, QUERIES), jnp.float32)
        for part in range(CHUNKS):
            weights = jnp.exp2(score_buf[part] - peak)
            prob_grad = lax.dot_general(
                values[rows(step + part, CHUNK), :],
                grad,
                contract_last,
                preferred_element_type=jnp.float32,
            )
            score_buf[part] = weights
            prob_buf[part] = prob_grad
            total = total + jnp.sum(weights, axis=0, keepdims=True)
            delta = delta + jnp.sum(weights * prob_grad, axis=0, keepdims=True)
        inverse = 1.0 / total
        delta = delta * inverse
        query_grad = jnp.zeros((HEAD_SIZE, QUERIES), jnp.float32)
        for part in range(CHUNKS):
            attention = score_buf[part] * inverse
            score_grad = (attention * (prob_buf[part] - delta)).astype(jnp.bfloat16)
            at = rows(step + part, CHUNK)
            value_sum[at, :] += jnp.dot(
                attention.astype(jnp.bfloat16), grad, preferred_element_type=jnp.float32
            )
            key_sum[at, :] += jnp.dot(score_grad, query, preferred_element_type=jnp.float32)
            query_grad = query_grad + jnp.dot(
                keys_t[step + part], score_grad, preferred_element_type=jnp.float32
            )
        query_stage[q_head, rows(step, QUERIES), :] = (score_scale * query_grad.T).astype(jnp.bfloat16)

    def query_local(q_head):
        return pltpu.make_async_copy(
            query_stage.at[q_head, rows(mine)],
            query_out.at[:, columns(2 * y + q_head)],
            query_recv.at[q_head, y],
        )

    def query_remote(q_head, block, device, home):
        return pltpu.make_async_remote_copy(
            src_ref=query_stage.at[q_head, rows(block)],
            dst_ref=query_out.at[:, columns(2 * home + q_head)],
            send_sem=query_send.at[q_head, block],
            recv_sem=query_recv.at[q_head, home],
            device_id=device,
            device_id_type=MESH,
        )

    def send_rows(step, local, remote):
        for block in (2 * step, 2 * step + 1):
            device = chip(block % 4 * 2 + core, block // 4)
            here = alone & (block == mine)

            @pl.when(here)
            def _():
                local()

            @pl.when(jnp.logical_not(here))
            def _():
                remote(block, device)

    def send_query(q_head, step):
        send_rows(
            step,
            lambda: query_local(q_head).start(),
            lambda block, device: query_remote(q_head, block, device, y).start(),
        )

    def back(which, step):
        return pltpu.make_async_remote_copy(
            src_ref=back_stage.at[which, rows(step, QUERIES)],
            dst_ref=back_landing.at[which, rows(step, QUERIES)],
            send_sem=back_send.at[which, step],
            recv_sem=back_recv.at[which, step],
            device_id=preceding,
            device_id_type=MESH,
        )

    wait_in(Q0)
    wait_in(G0)

    @pl.loop(0, STEPS)
    def _(step):
        compute(0, step)

        @pl.when(step < 2)
        def _():
            send_query(0, step)

    wait_in(Q1)
    wait_in(G1)
    for step in (2, 3):
        send_query(0, step)

    @pl.when(jnp.logical_not(below | first))
    def _():
        pl.semaphore_wait(seam_sem, 1)

    @pl.loop(0, STEPS)
    def _(step):
        compute(1, step)
        at = rows(step, QUERIES)
        back_stage[0, at, :] = (score_scale * key_sum[at, :]).astype(jnp.bfloat16)
        back_stage[1, at, :] = value_sum[at, :].astype(jnp.bfloat16)

        @pl.when(jnp.logical_not(first))
        def _():
            back(0, step).start()
            back(1, step).start()

        send_query(1, step)

    def own_out(which):
        return key_out if which == 0 else value_out

    def own_local(which):
        return pltpu.make_async_copy(
            own_stage.at[which, rows(mine)],
            own_out(which).at[:, columns(y)],
            own_recv.at[which, y],
        )

    def own_remote(which, block, device, home):
        return pltpu.make_async_remote_copy(
            src_ref=own_stage.at[which, rows(block)],
            dst_ref=own_out(which).at[:, columns(home)],
            send_sem=own_send.at[which, block],
            recv_sem=own_recv.at[which, home],
            device_id=device,
            device_id_type=MESH,
        )

    @pl.loop(0, STEPS)
    def _(turn):
        step = jnp.where(y < LINE // 2, turn + 1 - 2 * (turn % 2), turn)
        at = rows(step, QUERIES)
        own = rows(STEPS + step, QUERIES)

        @pl.when(jnp.logical_not(last))
        def _():
            back(0, step).wait_recv()
            back(1, step).wait_recv()

        for which, sums, scale in ((0, key_sum, score_scale), (1, value_sum, 1.0)):
            own_stage[which, at, :] = (
                scale * sums[own, :] + back_landing[which, at, :].astype(jnp.float32)
            ).astype(jnp.bfloat16)

        def local():
            own_local(0).start()
            own_local(1).start()

        def remote(block, device):
            own_remote(0, block, device, y).start()
            own_remote(1, block, device, y).start()

        send_rows(step, local, remote)

    @pl.when(jnp.logical_not(alone))
    def _():
        for kind in KINDS:
            remote_in(kind, *near_home, mine).wait_send()
        for which in (0, 1):
            query_remote(which, *near_owner, y).wait_send()
            own_remote(which, *near_owner, y).wait_send()

    for kind in KINDS:
        for home, device in homes:
            remote_in(kind, home, device, mine).wait_send()
    @pl.when(jnp.logical_not(last))
    def _():
        halo(0).wait_send()
        halo(1).wait_send()

    @pl.when(jnp.logical_not(first))
    def _():
        for step in range(STEPS):
            back(0, step).wait_send()
            back(1, step).wait_send()

    for which in (0, 1):
        for block, device in owners:
            query_remote(which, block, device, y).wait_send()
            own_remote(which, block, device, y).wait_send()
        for home, device in homes + [near_home]:
            query_remote(which, mine, device, home).wait_recv()
            own_remote(which, mine, device, home).wait_recv()


def store(query_from, key_from, value_from, query_to, key_to, value_to, done):
    pairs = ((query_from, query_to), (key_from, key_to), (value_from, value_to))
    copies = [
        pltpu.make_async_copy(source, target, done.at[index])
        for index, (source, target) in enumerate(pairs)
    ]
    for copy in copies:
        copy.start()
    for copy in copies:
        copy.wait()


def on_device(query_rows, key_rows, saved_value_rows, out_grad):
    dma = pltpu.SemaphoreType.DMA
    low, wide = jnp.bfloat16, jnp.float32
    anywhere = pl.BlockSpec(memory_space=pl.ANY)
    in_hbm = pl.BlockSpec(memory_space=pltpu.HBM)
    results = pl.pallas_call(
        kernel,
        out_shape=(
            pltpu.VMEM(query_rows.shape, low),
            pltpu.VMEM(key_rows.shape, low),
            pltpu.VMEM(saved_value_rows.shape, low),
        ),
        in_specs=[in_hbm] * 4,
        out_specs=(anywhere,) * 3,
        scratch_shapes=[
            pltpu.VMEM((2 * W, HEAD_SIZE), low),
            pltpu.VMEM((2 * W, HEAD_SIZE), low),
            pltpu.VMEM((2 * W // CHUNK, HEAD_SIZE, CHUNK), low),
            pltpu.VMEM((2, W, HEAD_SIZE), low),
            pltpu.VMEM((2, W, HEAD_SIZE), low),
            pltpu.VMEM((2 * W, HEAD_SIZE), wide),
            pltpu.VMEM((2 * W, HEAD_SIZE), wide),
            pltpu.VMEM((2, W, HEAD_SIZE), low),
            pltpu.VMEM((2, W, HEAD_SIZE), low),
            pltpu.VMEM((2, W, HEAD_SIZE), low),
            pltpu.VMEM((2, W, HEAD_SIZE), low),
            pltpu.VMEM((CHUNKS, CHUNK, QUERIES), wide),
            pltpu.VMEM((CHUNKS, CHUNK, QUERIES), wide),
            dma((6, LINE)),
            dma((6, BLOCKS)),
            dma((2,)),
            dma((2,)),
            dma((2, BLOCKS)),
            dma((2, LINE)),
            dma((2, STEPS)),
            dma((2, STEPS)),
            dma((2, BLOCKS)),
            dma((2, LINE)),
            pltpu.SemaphoreType.REGULAR,
            pltpu.SemaphoreType.REGULAR,
            pltpu.SemaphoreType.REGULAR,
            pltpu.SemaphoreType.REGULAR,
        ],
        compiler_params=pltpu.CompilerParams(
            collective_id=0, has_side_effects=True
        ),
        name="attention_backward",
    )(query_rows, key_rows, saved_value_rows, out_grad)
    in_vmem = pl.BlockSpec(memory_space=pltpu.VMEM)
    return pl.pallas_call(
        store,
        out_shape=tuple(jax.ShapeDtypeStruct(result.shape, low) for result in results),
        in_specs=[in_vmem] * 3,
        out_specs=(in_hbm,) * 3,
        scratch_shapes=[dma((3,))],
        compiler_params=pltpu.CompilerParams(vmem_limit_bytes=4 * 2**20),
        name="store",
    )(*results)


def solution(mesh):
    rows_split = P(("seq", "head"), None)
    return jax.shard_map(
        on_device,
        mesh=mesh,
        in_specs=(rows_split,) * 4,
        out_specs=(rows_split,) * 3,
        check_vma=False,
    )
```
